32 devices in a mesh: stream: 8 (over y, x, core), wall: 4 (over z).
Axes of the slice: x: 2, y: 2, z: 4, core: 2. Of those that a mesh axis runs over, the one named last changes fastest.
Arguments:
- velocity: float32 [3, 2, 768, 2048], P(None, None, 'wall', 'stream'), may hold values from -96 to 96
- viscosity: float32 [2, 768, 2048], P(None, 'wall', 'stream'), may hold values from 2 to 4000000
- y_coef: float32 [2, 768], P(None, 'wall'), may hold values from 0.05 to 0.25
Outputs:
- updated: float32 [3, 2, 768, 2048], P(None, None, 'wall', 'stream')
The draws below stay inside these ranges and needn't reach their ends.
All inputs are finite; a program needn't handle non-finite values.
Results may differ from the reference program's by a relative error of at most 0.0015.
Values sent between devices are 32-bit elements; how exact they have to be, the bound alone decides.
A program may use at most 64 MiB of HBM per device.

```python
import math
import jax
import jax.numpy as jnp
from jax import lax

COMPONENTS = 3
PLANES = 2
NX = 2048
NY = 768


def draw_viscosity(key, part):
    line_key = jax.random.fold_in(key, 11)
    cell_key = jax.random.fold_in(key, 23)
    line_low = math.log(4.0)
    cell_half = math.log(2.0)
    line_high = math.log(1000000.0)
    line_log = jax.random.uniform(line_key, (PLANES, NY, 1), jnp.float32, line_low, line_high)
    cell_log = jax.random.uniform(cell_key, (PLANES, NY, NX), jnp.float32, -cell_half, cell_half)
    return jnp.exp(line_log + cell_log).astype(jnp.float32)


def steps_of(key, dims, split, smallest, high):
    def one(position, parts):
        heights = jax.random.uniform(jax.random.fold_in(jax.random.fold_in(key, 6), position), (parts,), jnp.float32, smallest / len(split), high / len(split))
        return jnp.repeat(jnp.exp(heights), dims[position] // parts).reshape((-1,) + (1,) * (len(dims) - position - 1))

    gain = one(*split[0])
    for cut in split[1:]:
        gain = gain * one(*cut)
    return gain


def centred(rng, extent, scale, limit, pieces=(), held_as=jnp.bfloat16):
    level = steps_of(rng, extent, pieces, -0.22, 0.18) if pieces else 1.0
    values = jax.random.normal(rng, extent, jnp.float32) * scale * level
    return jnp.minimum(jnp.maximum(values, -limit), limit).astype(held_as)


def setup_inputs(seed: int = 0) -> dict:
    streams_of = jax.random.split(jax.random.key(seed), 4)
    velocity = centred(streams_of[0], (COMPONENTS, PLANES, NY, NX), 16.0, 96.0, ((2, 4), (3, 8)), jnp.float32)
    viscosity = draw_viscosity(jax.random.fold_in(streams_of[3], 71), 0)
    y_coef = jnp.clip(jnp.exp(math.log(0.25) - 1.609438 * jax.random.uniform(streams_of[2], (2, NY), jnp.float32) ** steps_of(streams_of[2], (2, NY), ((1, 4),), -0.2, 0.2)), 0.05, 0.25)
    return {"velocity": velocity, "viscosity": viscosity, "y_coef": y_coef}


def thomas_sweep(lower_t, diag_t, upper_t, source_t):
    def forward(carry, entry):
        ratio_prev, value_prev = carry
        low_e, dia_e, upp_e, src_e = entry
        denom = dia_e - low_e * ratio_prev
        ratio_new = upp_e / denom
        value_new = (src_e - low_e[None] * value_prev) / denom[None]
        return (ratio_new, value_new), (ratio_new, value_new)

    start = (jnp.zeros_like(diag_t[0]), jnp.zeros_like(source_t[0]))
    _, (ratios, values) = lax.scan(forward, start, (lower_t, diag_t, upper_t, source_t))

    def backward(following, entry):
        ratio_e, value_e = entry
        current = value_e - ratio_e[None] * following
        return current, current

    _, solved = lax.scan(backward, jnp.zeros_like(source_t[0]), (ratios, values), reverse=True)
    return solved


def solve_plane(inputs):
    lower_p, diag_p, upper_p, source_p = inputs
    lower_t = lower_p.T
    diag_t = diag_p.T
    upper_t = upper_p.T
    source_t = jnp.transpose(source_p, (2, 0, 1))
    gamma = -diag_t[0]
    last_diag = diag_t[-1] - lower_t[0] * upper_t[-1] / gamma
    diag_mod = jnp.concatenate([(diag_t[0] - gamma)[None], diag_t[1:-1], last_diag[None]], axis=0)
    lower_mod = jnp.concatenate([jnp.zeros_like(lower_t[:1]), lower_t[1:]], axis=0)
    middle = jnp.zeros_like(diag_t[1:-1])
    spike = jnp.concatenate([gamma[None], middle, upper_t[-1][None]], axis=0)[:, None, :]
    solved = thomas_sweep(lower_mod, diag_mod, upper_t, jnp.concatenate([source_t, spike], axis=1))
    plain = solved[:, :3]
    spiked = solved[:, 3:]
    factor = (lower_t[0] / gamma)
    plain_dot = plain[0] + factor[None] * plain[-1]
    spiked_dot = spiked[0] + factor[None] * spiked[-1]
    result = plain - spiked * (plain_dot / (1.0 + spiked_dot))[None]
    return jnp.transpose(result, (1, 2, 0))


def reference(velocity, viscosity, y_coef):
    padded = jnp.pad(velocity, ((0, 0), (0, 0), (1, 1), (0, 0)))
    coef_up = y_coef[0][None, None, :, None]
    coef_down = y_coef[1][None, None, :, None]
    source = velocity + coef_up * (padded[:, :, 2:] - velocity) - coef_down * (velocity - padded[:, :, :-2])
    stiffness = viscosity
    lower = -0.5 * (jnp.roll(stiffness, 1, axis=-1) + stiffness)
    upper = -0.5 * (stiffness + jnp.roll(stiffness, -1, axis=-1))
    diagonal = 1.0 - lower - upper
    planes_out = lax.map(solve_plane, (lower, diagonal, upper, jnp.transpose(source, (1, 0, 2, 3))))
    return jnp.transpose(planes_out, (1, 0, 2, 3))
```

```python
import functools

import jax
import jax.numpy as jnp
from jax import lax
from jax.experimental import pallas as pl
from jax.experimental.pallas import tpu as pltpu
from jax.sharding import PartitionSpec as P

SEGMENTS = 8
LANES = 128
MESH = pl.DeviceIdType.MESH


def up8(rows):
    return -(-rows // 8) * 8


def join_matrix(a, b, link):
    a00, a0l, all_ = a
    b00, b0l, bll = b
    gain = link / (1.0 + link * (all_ + b00))
    left = gain * a0l
    right = gain * b0l
    return (a00 - left * a0l, left * b0l, bll - right * b0l), (gain, left, right)


def join_values(a, b, weights):
    _, left, right = weights
    jump = [al - b0 for al, b0 in zip(a[1], b[0])]
    first = [a0 - left * j for a0, j in zip(a[0], jump)]
    last = [bl + right * j for bl, j in zip(b[1], jump)]
    return (first, last), jump


def join_tree(blocks):
    levels = []
    while len(blocks) > 1:
        merged, weights = [], []
        for i in range(0, len(blocks) - 1, 2):
            (ma, fa, la), (mb, fb, lb) = blocks[i], blocks[i + 1]
            m, w = join_matrix(ma, mb, 0.5 * (la + fb))
            merged.append((m, fa, lb))
            weights.append(w)
        if len(blocks) % 2:
            merged.append(blocks[-1])
        levels.append(weights)
        blocks = merged
    return blocks[0], levels


def value_tree(values, levels):
    jumps = []
    for weights in levels:
        merged, jump = [], []
        for i, w in enumerate(weights):
            v, j = join_values(values[2 * i], values[2 * i + 1], w)
            merged.append(v)
            jump.append(j)
        if len(values) % 2:
            merged.append(values[-1])
        jumps.append(jump)
        values = merged
    return values[0], jumps


def down_tree(levels, jumps, inflow, outflow):
    flows = [(inflow, outflow)]
    for depth in reversed(range(len(levels))):
        spread = []
        for i, (gain, left, right) in enumerate(levels[depth]):
            fin, fout = flows[i]
            middle = None
            for term, weight in ((fin, left), (fout, right)):
                if term is not None:
                    part = weight if isinstance(term, float) else term * weight
                    middle = part if middle is None else middle + part
            if jumps is not None:
                part = gain * jumps[depth][i]
                middle = part if middle is None else middle + part
            spread += [(fin, middle), (middle, fout)]
        flows = spread
    return flows


def kernel(devices, wall_devices, planes, vel, visc, coef, out,
           rows_out, rows_in, stiff_t, src, src_t, ratio_s, inv_s, head_s, y_s, seg, flow,
           sol_t, sol, coef_s, ring_s, msg_a, msg_b, got_a, got_b,
           wall_send, wall_recv, a_send, a_recv, b_send, b_recv):
    components, lines, cells = vel.shape
    rows = lines // planes
    groups = lines // LANES
    length = cells // SEGMENTS
    me = lax.axis_index("stream")
    wall = lax.axis_index("wall")
    has_below = wall > 0
    has_above = wall < wall_devices - 1

    barrier = pltpu.get_barrier_semaphore()
    for d in range(1, devices):
        pl.semaphore_signal(barrier, inc=1, device_id={"stream": lax.rem(me + d, devices)}, device_id_type=MESH)

    @pl.when(has_below)
    def _():
        pl.semaphore_signal(barrier, inc=1, device_id={"wall": wall - 1}, device_id_type=MESH)

    @pl.when(has_above)
    def _():
        pl.semaphore_signal(barrier, inc=1, device_id={"wall": wall + 1}, device_id_type=MESH)

    for c in range(components):
        for p in range(planes):
            at = c * planes + p
            rows_out[0, at : at + 1, :] = vel[c, p * rows + rows - 1 : p * rows + rows, :]
            rows_out[1, at : at + 1, :] = vel[c, p * rows : p * rows + 1, :]

    beside = jnp.where(has_below, 1, 0) + jnp.where(has_above, 1, 0)
    pl.semaphore_wait(barrier, devices - 1 + beside)

    def wall_copy(side, target):
        return pltpu.make_async_remote_copy(
            src_ref=rows_out.at[side], dst_ref=rows_in.at[side],
            send_sem=wall_send.at[side], recv_sem=wall_recv.at[side],
            device_id={"wall": target}, device_id_type=MESH)

    @pl.when(has_above)
    def _():
        wall_copy(0, wall + 1).start()

    @pl.when(has_below)
    def _():
        wall_copy(1, wall - 1).start()

    @pl.when(jnp.logical_not(has_below))
    def _():
        rows_in[0] = jnp.zeros(rows_in.shape[1:], jnp.float32)

    @pl.when(jnp.logical_not(has_above))
    def _():
        rows_in[1] = jnp.zeros(rows_in.shape[1:], jnp.float32)

    def ring_copy(d, source, target, send, recv):
        return pltpu.make_async_remote_copy(
            src_ref=source, dst_ref=target.at[d - 1],
            send_sem=send.at[d - 1], recv_sem=recv.at[d - 1],
            device_id={"stream": lax.rem(me + d, devices)}, device_id_type=MESH)

    def at_position(i):
        return pl.ds(i, SEGMENTS, stride=length)

    def put_segments(slot, value):
        for g in range(groups):
            seg[slot, pl.ds(g, SEGMENTS, stride=8), :] = value[g]

    def take_segment(slot, s):
        return seg[slot, s * 8 : s * 8 + groups, :]

    for g in range(groups):
        stiff_t[g] = visc[g * LANES : (g + 1) * LANES, :].T

    one = jnp.ones((groups, SEGMENTS, LANES), jnp.float32)
    excess = one
    reach = one
    first_first = jnp.zeros_like(one)
    stiff = stiff_t[:, at_position(0), :]
    first_stiff = stiff
    for i in range(length):
        if i < length - 1:
            following = stiff_t[:, at_position(i + 1), :]
            link = 0.5 * (stiff + following)
            stiff = following
            inv = 1.0 / (excess + link)
            ratio = link * inv
            ratio_s[i] = ratio
        else:
            inv = 1.0 / excess
        head = reach * inv
        inv_s[i] = inv
        head_s[i] = head
        first_first = first_first + head * reach
        if i < length - 1:
            excess = 1.0 + ratio * excess
            reach = reach * ratio
    for slot, value in enumerate((first_first, head, inv, first_stiff, stiff)):
        put_segments(slot, value)
    blocks = []
    for s in range(SEGMENTS):
        v = [take_segment(slot, s) for slot in range(5)]
        blocks.append((tuple(v[:3]), v[3], v[4]))
    mine, levels = join_tree(blocks)
    for q, value in enumerate(mine[0] + (mine[1], mine[2])):
        msg_a[q * groups : (q + 1) * groups, :] = value
    for d in range(1, devices):
        ring_copy(d, msg_a, got_a, a_send, a_recv).start()

    coef_s[...] = jnp.zeros(coef_s.shape, jnp.float32)
    coef_s[0:2, 0:rows] = coef[...]
    turned = coef_s[...].T
    toward_up = turned[0:rows, 0:1]
    toward_down = turned[0:rows, 1:2]
    keep = 1.0 - toward_up - toward_down
    row_of = lax.broadcasted_iota(jnp.int32, (rows, cells), 0)

    @pl.when(has_below)
    def _():
        wall_copy(0, wall).wait_recv()

    @pl.when(has_above)
    def _():
        wall_copy(1, wall).wait_recv()

    for c in range(components):
        for p in range(planes):
            at = c * planes + p
            v = vel[c, p * rows : (p + 1) * rows, :]
            above = jnp.where(row_of == rows - 1, rows_in[1, at : at + 1, :], pltpu.roll(v, rows - 1, 0))
            below = jnp.where(row_of == 0, rows_in[0, at : at + 1, :], pltpu.roll(v, 1, 0))
            src[c, p * rows : (p + 1) * rows, :] = v + toward_up * (above - v) - toward_down * (v - below)
        for g in range(groups):
            src_t[c, g] = src[c, g * LANES : (g + 1) * LANES, :].T

    y = [None] * components
    first = [None] * components
    for i in range(length):
        head = head_s[i]
        for c in range(components):
            f = src_t[c, :, at_position(i), :]
            y[c] = f if i == 0 else f + ratio_s[i - 1] * y[c]
            y_s[c, i] = y[c]
            first[c] = head * y[c] if i == 0 else first[c] + head * y[c]
    inv = inv_s[length - 1]
    for c in range(components):
        put_segments(c, first[c])
        put_segments(components + c, inv * y[c])
    values = []
    for s in range(SEGMENTS):
        v = [take_segment(slot, s) for slot in range(2 * components)]
        values.append((v[:components], v[components:]))
    own, jumps = value_tree(values, levels)
    for q, value in enumerate(own[0] + own[1]):
        msg_b[q * groups : (q + 1) * groups, :] = value
    for d in range(1, devices):
        ring_copy(d, msg_b, got_b, b_send, b_recv).start()

    fields = components + 2
    zero = jnp.zeros((groups, LANES), jnp.float32)
    unit = jnp.ones((groups, LANES), jnp.float32)
    for f in range(fields):
        if f < components:
            picked = [[j[f] for j in level] for level in jumps]
            flows = down_tree(levels, picked, None, None)
        elif f == components:
            flows = down_tree(levels, None, 1.0, None)
        else:
            flows = down_tree(levels, None, None, 1.0)
        for s, (fin, fout) in enumerate(flows):
            for side, term in enumerate((fin, fout)):
                term = zero if term is None else unit if isinstance(term, float) else term
                seg[2 * f + side, s * 8 : s * 8 + groups, :] = term
    fin, fout = [], []
    for f in range(fields):
        for slot, into in ((2 * f, fin), (2 * f + 1, fout)):
            into.append(jnp.stack([seg[slot, pl.ds(g, SEGMENTS, stride=8), :] for g in range(groups)]))
    now = [None] * fields
    for i in reversed(range(length)):
        head = head_s[i]
        inv = inv_s[i]
        if i < length - 1:
            ratio = ratio_s[i]
        for f in range(fields):
            value = fin[f] * head
            if f < components:
                value = value + y_s[f, i] * inv
            if i < length - 1:
                value = value + ratio * now[f]
            else:
                value = value - fout[f] * inv
            now[f] = value
            sol_t[f, :, at_position(i), :] = value
    for f in range(fields):
        for g in range(groups):
            sol[f, g * LANES : (g + 1) * LANES, :] = sol_t[f, g].T

    for d in range(1, devices):
        ring_copy(d, msg_a, got_a, a_send, a_recv).wait()
    others = []
    for t in range(1, devices):
        slot = devices - t - 1
        v = [got_a[slot, q * groups : (q + 1) * groups, :] for q in range(5)]
        others.append((tuple(v[:3]), v[3], v[4]))
    rest, ring_levels = join_tree(others)
    (m00, m0l, mll), m_first, m_last = mine
    (b00, b0l, bll), b_first, b_last = rest
    out_diag = 2.0 / (m_last + b_first) + mll + b00
    in_diag = 2.0 / (b_last + m_first) + bll + m00
    cross = m0l + b0l
    det = 1.0 / (out_diag * in_diag - cross * cross)

    for d in range(1, devices):
        ring_copy(d, msg_b, got_b, b_send, b_recv).wait()
    theirs = []
    for t in range(1, devices):
        slot = devices - t - 1
        v = [got_b[slot, q * groups : (q + 1) * groups, :] for q in range(2 * components)]
        theirs.append((v[:components], v[components:]))
    tail, _ = value_tree(theirs, ring_levels)
    for c in range(components):
        gap_out = own[1][c] - tail[0][c]
        gap_in = tail[1][c] - own[0][c]
        outflow = (in_diag * gap_out + cross * gap_in) * det
        inflow = (out_diag * gap_in + cross * gap_out) * det
        for g in range(groups):
            flow[g, c : c + 1, :] = inflow[g : g + 1]
            flow[g, components + c : components + c + 1, :] = outflow[g : g + 1]

    for g in range(groups):
        span = slice(g * LANES, (g + 1) * LANES)
        columns = flow[g].T
        from_left = sol[components, span, :]
        from_right = sol[components + 1, span, :]
        for c in range(components):
            out[c, span, :] = (
                sol[c, span, :]
                + columns[:, c : c + 1] * from_left
                + columns[:, components + c : components + c + 1] * from_right
            )

    @pl.when(has_above)
    def _():
        wall_copy(0, wall + 1).wait_send()

    @pl.when(has_below)
    def _():
        wall_copy(1, wall - 1).wait_send()


def shards(devices, wall_devices, velocity, viscosity, y_coef):
    components, planes, rows, cells = velocity.shape
    lines = planes * rows
    groups = lines // LANES
    length = cells // SEGMENTS
    fields = components + 2
    f32 = jnp.float32
    edge = up8(components * planes)
    rows_a, rows_b = up8(5 * groups), up8(2 * components * groups)
    peers = devices - 1
    tiles = (groups, SEGMENTS, LANES)
    flipped = (groups, cells, LANES)
    vmem = pl.BlockSpec(memory_space=pltpu.VMEM)
    result = pl.pallas_call(
        functools.partial(kernel, devices, wall_devices, planes),
        out_shape=jax.ShapeDtypeStruct((components, lines, cells), f32),
        in_specs=[vmem] * 3,
        out_specs=vmem,
        scratch_shapes=[
            pltpu.VMEM((2, edge, cells), f32),
            pltpu.VMEM((2, edge, cells), f32),
            pltpu.VMEM(flipped, f32),
            pltpu.VMEM((components, lines, cells), f32),
            pltpu.VMEM((components,) + flipped, f32),
            pltpu.VMEM((length,) + tiles, f32),
            pltpu.VMEM((length,) + tiles, f32),
            pltpu.VMEM((length,) + tiles, f32),
            pltpu.VMEM((components, length) + tiles, f32),
            pltpu.VMEM((2 * fields, SEGMENTS * 8, LANES), f32),
            pltpu.VMEM((groups, up8(2 * components), LANES), f32),
            pltpu.VMEM((fields,) + flipped, f32),
            pltpu.VMEM((fields, lines, cells), f32),
            pltpu.VMEM((8, -(-rows // LANES) * LANES), f32),
            pltpu.VMEM((8, LANES), f32),
            pltpu.VMEM((rows_a, LANES), f32),
            pltpu.VMEM((rows_b, LANES), f32),
            pltpu.VMEM((peers, rows_a, LANES), f32),
            pltpu.VMEM((peers, rows_b, LANES), f32),
            pltpu.SemaphoreType.DMA((2,)),
            pltpu.SemaphoreType.DMA((2,)),
            pltpu.SemaphoreType.DMA((peers,)),
            pltpu.SemaphoreType.DMA((peers,)),
            pltpu.SemaphoreType.DMA((peers,)),
            pltpu.SemaphoreType.DMA((peers,)),
        ],
        compiler_params=pltpu.CompilerParams(
            collective_id=0, has_side_effects=True, vmem_limit_bytes=40 * 1024 * 1024
        ),
        name="implicit_lines",
    )(
        velocity.reshape(components, lines, cells),
        viscosity.reshape(lines, cells),
        y_coef,
    )
    return result.reshape(velocity.shape)


def solution(mesh):
    placed = (P(None, None, "wall", "stream"), P(None, "wall", "stream"), P(None, "wall"))
    return jax.shard_map(
        functools.partial(shards, mesh.shape["stream"], mesh.shape["wall"]),
        mesh=mesh,
        in_specs=placed,
        out_specs=P(None, None, "wall", "stream"),
        check_vma=False,
    )
```

```python
import functools

import jax
import jax.numpy as jnp
from jax import lax
from jax.experimental import pallas as pl
from jax.experimental.pallas import tpu as pltpu
from jax.sharding import PartitionSpec as P

SEGMENTS = 8
LANES = 128
MESH = pl.DeviceIdType.MESH


def up8(rows):
    return -(-rows // 8) * 8


def join_matrix(a, b, link):
    a00, a0l, all_ = a
    b00, b0l, bll = b
    gain = link / (1.0 + link * (all_ + b00))
    left = gain * a0l
    right = gain * b0l
    return (a00 - left * a0l, left * b0l, bll - right * b0l), (gain, left, right)


def join_values(a, b, weights):
    _, left, right = weights
    jump = [al - b0 for al, b0 in zip(a[1], b[0])]
    first = [a0 - left * j for a0, j in zip(a[0], jump)]
    last = [bl + right * j for bl, j in zip(b[1], jump)]
    return (first, last), jump


def join_tree(blocks):
    levels = []
    while len(blocks) > 1:
        merged, weights = [], []
        for i in range(0, len(blocks) - 1, 2):
            (ma, fa, la), (mb, fb, lb) = blocks[i], blocks[i + 1]
            m, w = join_matrix(ma, mb, 0.5 * (la + fb))
            merged.append((m, fa, lb))
            weights.append(w)
        if len(blocks) % 2:
            merged.append(blocks[-1])
        levels.append(weights)
        blocks = merged
    return blocks[0], levels


def value_tree(values, levels):
    jumps = []
    for weights in levels:
        merged, jump = [], []
        for i, w in enumerate(weights):
            v, j = join_values(values[2 * i], values[2 * i + 1], w)
            merged.append(v)
            jump.append(j)
        if len(values) % 2:
            merged.append(values[-1])
        jumps.append(jump)
        values = merged
    return values[0], jumps


def down_tree(levels, jumps, inflow, outflow):
    flows = [(inflow, outflow)]
    for depth in reversed(range(len(levels))):
        spread = []
        for i, (gain, left, right) in enumerate(levels[depth]):
            fin, fout = flows[i]
            middle = None
            for term, weight in ((fin, left), (fout, right)):
                if term is not None:
                    part = weight if isinstance(term, float) else term * weight
                    middle = part if middle is None else middle + part
            if jumps is not None:
                part = gain * jumps[depth][i]
                middle = part if middle is None else middle + part
            spread += [(fin, middle), (middle, fout)]
        flows = spread
    return flows


def kernel(devices, wall_devices, planes, vel_hbm, visc_hbm, coef_hbm, out,
           vel, visc, coef, rows_out, rows_in, rim, stiff_t, src, src_t, rim_t, ratio_s, inv_s, head_s,
           y_s, rim_y, seg, flow, sol_t, sol, coef_s, msg_a, msg_b, msg_c, got_a, got_b, got_c, load_sem,
           wall_send, wall_recv, a_send, a_recv, b_send, b_recv, c_send, c_recv):
    components, lines, cells = vel.shape
    rows = lines // planes
    groups = lines // LANES
    length = cells // SEGMENTS
    me = lax.axis_index("stream")
    wall = lax.axis_index("wall")
    has_below = wall > 0
    has_above = wall < wall_devices - 1

    barrier = pltpu.get_barrier_semaphore()
    for d in range(1, devices):
        pl.semaphore_signal(barrier, inc=1, device_id={"stream": lax.rem(me + d, devices)}, device_id_type=MESH)

    @pl.when(has_below)
    def _():
        pl.semaphore_signal(barrier, inc=1, device_id={"wall": wall - 1}, device_id_type=MESH)

    @pl.when(has_above)
    def _():
        pl.semaphore_signal(barrier, inc=1, device_id={"wall": wall + 1}, device_id_type=MESH)

    loads = [
        pltpu.make_async_copy(source, target, load_sem.at[i])
        for i, (source, target) in enumerate(((visc_hbm, visc), (vel_hbm, vel), (coef_hbm, coef)))
    ]
    for load in loads:
        load.start()
    bounds = [(c * planes + p, c, p * rows, (p + 1) * rows - 1) for c in range(components) for p in range(planes)]
    loads[0].wait()
    rim[...] = jnp.ones(rim.shape, jnp.float32)
    for at, c, low, high in bounds:
        rim[at : at + 1, :] = visc[low : low + 1, :]
        rim[8 + at : 9 + at, :] = visc[high : high + 1, :]
    for g in range(groups):
        stiff_t[g] = visc[g * LANES : (g + 1) * LANES, :].T
    stiff_t[groups] = rim[...].T

    loads[1].wait()
    for at, c, low, high in bounds:
        rows_out[0, at : at + 1, :] = vel[c, high : high + 1, :]
        rows_out[1, at : at + 1, :] = vel[c, low : low + 1, :]
    beside = jnp.where(has_below, 1, 0) + jnp.where(has_above, 1, 0)
    pl.semaphore_wait(barrier, devices - 1 + beside)

    def wall_copy(side, target):
        return pltpu.make_async_remote_copy(
            src_ref=rows_out.at[side], dst_ref=rows_in.at[side],
            send_sem=wall_send.at[side], recv_sem=wall_recv.at[side],
            device_id={"wall": target}, device_id_type=MESH)

    @pl.when(has_above)
    def _():
        wall_copy(0, wall + 1).start()

    @pl.when(has_below)
    def _():
        wall_copy(1, wall - 1).start()

    @pl.when(jnp.logical_not(has_below))
    def _():
        rows_in[0] = jnp.zeros(rows_in.shape[1:], jnp.float32)

    @pl.when(jnp.logical_not(has_above))
    def _():
        rows_in[1] = jnp.zeros(rows_in.shape[1:], jnp.float32)

    def ring_copy(d, source, target, send, recv):
        return pltpu.make_async_remote_copy(
            src_ref=source, dst_ref=target.at[d - 1],
            send_sem=send.at[d - 1], recv_sem=recv.at[d - 1],
            device_id={"stream": lax.rem(me + d, devices)}, device_id_type=MESH)

    def at_position(i):
        return pl.ds(i, SEGMENTS, stride=length)

    every = groups + 1

    def put_segments(slot, value, first_group=0):
        for g in range(value.shape[0]):
            seg[slot, pl.ds(first_group + g, SEGMENTS, stride=8), :] = value[g]

    def take_segment(slot, s, span=slice(0, groups)):
        return seg[slot, s * 8 + span.start : s * 8 + span.stop, :]

    one = jnp.ones((every, SEGMENTS, LANES), jnp.float32)
    excess = one
    reach = one
    first_first = jnp.zeros_like(one)
    stiff = stiff_t[:, at_position(0), :]
    first_stiff = stiff
    for i in range(length):
        if i < length - 1:
            following = stiff_t[:, at_position(i + 1), :]
            link = 0.5 * (stiff + following)
            stiff = following
            inv = 1.0 / (excess + link)
            ratio = link * inv
            ratio_s[i] = ratio
        else:
            inv = 1.0 / excess
        head = reach * inv
        inv_s[i] = inv
        head_s[i] = head
        first_first = first_first + head * reach
        if i < length - 1:
            excess = 1.0 + ratio * excess
            reach = reach * ratio
    for slot, value in enumerate((first_first, head, inv, first_stiff, stiff)):
        put_segments(slot, value)
    blocks = []
    for s in range(SEGMENTS):
        v = [take_segment(slot, s, slice(0, every)) for slot in range(5)]
        blocks.append((tuple(v[:3]), v[3], v[4]))
    mine, levels = join_tree(blocks)
    for q, value in enumerate(mine[0] + (mine[1], mine[2])):
        msg_a[q * every : (q + 1) * every, :] = value
    for d in range(1, devices):
        ring_copy(d, msg_a, got_a, a_send, a_recv).start()

    def part(levels, span):
        return [[tuple(w[span] for w in weights) for weights in level] for level in levels]

    main, last = slice(0, groups), slice(groups, every)
    main_levels, rim_levels = part(levels, main), part(levels, last)
    loads[2].wait()
    coef_s[...] = jnp.zeros(coef_s.shape, jnp.float32)
    coef_s[0:2, 0:rows] = coef[...]
    turned = coef_s[...].T
    toward_up = turned[0:rows, 0:1]
    toward_down = turned[0:rows, 1:2]
    keep = 1.0 - toward_up - toward_down
    row_of = lax.broadcasted_iota(jnp.int32, (rows, cells), 0)

    for c in range(components):
        for p in range(planes):
            v = vel[c, p * rows : (p + 1) * rows, :]
            above = jnp.where(row_of == rows - 1, 0.0, pltpu.roll(v, rows - 1, 0))
            below = jnp.where(row_of == 0, 0.0, pltpu.roll(v, 1, 0))
            src[c, p * rows : (p + 1) * rows, :] = v + toward_up * (above - v) - toward_down * (v - below)
        for g in range(groups):
            src_t[c, g] = src[c, g * LANES : (g + 1) * LANES, :].T

    y = [None] * components
    first = [None] * components
    for i in range(length):
        head = head_s[i, main]
        for c in range(components):
            f = src_t[c, :, at_position(i), :]
            y[c] = f if i == 0 else f + ratio_s[i - 1, main] * y[c]
            y_s[c, i] = y[c]
            first[c] = head * y[c] if i == 0 else first[c] + head * y[c]
    inv = inv_s[length - 1, main]
    for c in range(components):
        put_segments(c, first[c])
        put_segments(components + c, inv * y[c])
    values = []
    for s in range(SEGMENTS):
        v = [take_segment(slot, s) for slot in range(2 * components)]
        values.append((v[:components], v[components:]))
    own, jumps = value_tree(values, main_levels)
    for q, value in enumerate(own[0] + own[1]):
        msg_b[q * groups : (q + 1) * groups, :] = value
    for d in range(1, devices):
        ring_copy(d, msg_b, got_b, b_send, b_recv).start()

    @pl.when(has_below)
    def _():
        wall_copy(0, wall).wait_recv()

    @pl.when(has_above)
    def _():
        wall_copy(1, wall).wait_recv()

    rim[0:8, :] = rows_in[0] * turned[0:1, 1:2]
    rim[8:16, :] = rows_in[1] * turned[rows - 1 : rows, 0:1]
    rim_t[...] = rim[...].T
    for i in range(length):
        f = rim_t[at_position(i), :]
        head = head_s[i, groups]
        edge = f if i == 0 else f + ratio_s[i - 1, groups] * edge
        rim_y[i] = edge
        edge_first = head * edge if i == 0 else edge_first + head * edge
    put_segments(0, edge_first[None], groups)
    put_segments(1, (inv_s[length - 1, groups] * edge)[None], groups)
    values = []
    for s in range(SEGMENTS):
        v = [take_segment(slot, s, last) for slot in range(2)]
        values.append((v[:1], v[1:]))
    rim_own, rim_jumps = value_tree(values, rim_levels)
    msg_c[0:1, :] = rim_own[0][0]
    msg_c[1:2, :] = rim_own[1][0]
    for d in range(1, devices):
        ring_copy(d, msg_c, got_c, c_send, c_recv).start()

    fields = components + 2
    zero = jnp.zeros((groups, LANES), jnp.float32)
    unit = jnp.ones((groups, LANES), jnp.float32)
    for f in range(fields):
        if f < components:
            picked = [[j[f] for j in level] for level in jumps]
            flows = down_tree(main_levels, picked, None, None)
        elif f == components:
            flows = down_tree(main_levels, None, 1.0, None)
        else:
            flows = down_tree(main_levels, None, None, 1.0)
        for s, (fin, fout) in enumerate(flows):
            for side, term in enumerate((fin, fout)):
                term = zero if term is None else unit if isinstance(term, float) else term
                seg[2 * f + side, s * 8 : s * 8 + groups, :] = term
    fin, fout = [], []
    for f in range(fields):
        for slot, into in ((2 * f, fin), (2 * f + 1, fout)):
            into.append(jnp.stack([seg[slot, pl.ds(g, SEGMENTS, stride=8), :] for g in range(groups)]))
    picked = [[j[0] for j in level] for level in rim_jumps]
    for s, terms in enumerate(down_tree(rim_levels, picked, None, None)):
        for side, term in enumerate(terms):
            term = jnp.zeros((1, LANES), jnp.float32) if term is None else term
            seg[side, s * 8 + groups : s * 8 + every, :] = term
    rim_fin, rim_fout = (seg[side, pl.ds(groups, SEGMENTS, stride=8), :] for side in range(2))
    for i in reversed(range(length)):
        value = rim_fin * head_s[i, groups] + rim_y[i] * inv_s[i, groups]
        if i < length - 1:
            value = value + ratio_s[i, groups] * edge
        else:
            value = value - rim_fout * inv_s[i, groups]
        edge = value
        rim_t[at_position(i), :] = edge
    rim[...] = rim_t[...].T
    now = [None] * fields
    for i in reversed(range(length)):
        head = head_s[i, main]
        inv = inv_s[i, main]
        if i < length - 1:
            ratio = ratio_s[i, main]
        for f in range(fields):
            value = fin[f] * head
            if f < components:
                value = value + y_s[f, i] * inv
            if i < length - 1:
                value = value + ratio * now[f]
            else:
                value = value - fout[f] * inv
            now[f] = value
            sol_t[f, :, at_position(i), :] = value
    for f in range(fields):
        for g in range(groups):
            sol[f, g * LANES : (g + 1) * LANES, :] = sol_t[f, g].T

    for d in range(1, devices):
        ring_copy(d, msg_a, got_a, a_send, a_recv).wait()
    others = []
    for t in range(1, devices):
        slot = devices - t - 1
        v = [got_a[slot, q * every : (q + 1) * every, :] for q in range(5)]
        others.append((tuple(v[:3]), v[3], v[4]))
    rest, ring_levels = join_tree(others)
    (m00, m0l, mll), m_first, m_last = mine
    (b00, b0l, bll), b_first, b_last = rest
    out_diag = 2.0 / (m_last + b_first) + mll + b00
    in_diag = 2.0 / (b_last + m_first) + bll + m00
    cross = m0l + b0l
    det = 1.0 / (out_diag * in_diag - cross * cross)

    def end_flows(mine_ends, other_ends, span):
        gap_out = mine_ends[1] - other_ends[0]
        gap_in = other_ends[1] - mine_ends[0]
        outflow = (in_diag[span] * gap_out + cross[span] * gap_in) * det[span]
        inflow = (out_diag[span] * gap_in + cross[span] * gap_out) * det[span]
        return inflow, outflow

    for d in range(1, devices):
        ring_copy(d, msg_b, got_b, b_send, b_recv).wait()
    theirs = []
    for t in range(1, devices):
        slot = devices - t - 1
        v = [got_b[slot, q * groups : (q + 1) * groups, :] for q in range(2 * components)]
        theirs.append((v[:components], v[components:]))
    tail, _ = value_tree(theirs, part(ring_levels, main))
    for c in range(components):
        inflow, outflow = end_flows((own[0][c], own[1][c]), (tail[0][c], tail[1][c]), main)
        for g in range(groups):
            flow[g, c : c + 1, :] = inflow[g : g + 1]
            flow[g, components + c : components + c + 1, :] = outflow[g : g + 1]

    for g in range(groups):
        span = slice(g * LANES, (g + 1) * LANES)
        columns = flow[g].T
        from_left = sol[components, span, :]
        from_right = sol[components + 1, span, :]
        for c in range(components):
            out[c, span, :] = (
                sol[c, span, :]
                + columns[:, c : c + 1] * from_left
                + columns[:, components + c : components + c + 1] * from_right
            )

    for d in range(1, devices):
        ring_copy(d, msg_c, got_c, c_send, c_recv).wait()
    theirs = []
    for t in range(1, devices):
        slot = devices - t - 1
        theirs.append(([got_c[slot, 0:1, :]], [got_c[slot, 1:2, :]]))
    tail, _ = value_tree(theirs, part(ring_levels, last))
    inflow, outflow = end_flows((rim_own[0][0], rim_own[1][0]), (tail[0][0], tail[1][0]), last)
    flow[0, 0:1, :] = inflow
    flow[0, 1:2, :] = outflow
    columns = flow[0].T
    for at, c, low, high in bounds:
        for e, r in ((at, low), (8 + at, high)):
            out[c, r : r + 1, :] = (
                out[c, r : r + 1, :]
                + rim[e : e + 1, :]
                + columns[e : e + 1, 0:1] * sol[components, r : r + 1, :]
                + columns[e : e + 1, 1:2] * sol[components + 1, r : r + 1, :]
            )

    @pl.when(has_above)
    def _():
        wall_copy(0, wall + 1).wait_send()

    @pl.when(has_below)
    def _():
        wall_copy(1, wall - 1).wait_send()


def shards(devices, wall_devices, velocity, viscosity, y_coef):
    components, planes, rows, cells = velocity.shape
    lines = planes * rows
    groups = lines // LANES
    length = cells // SEGMENTS
    fields = components + 2
    f32 = jnp.float32
    every = groups + 1
    rows_a, rows_b = up8(5 * every), up8(2 * components * groups)
    peers = devices - 1
    tiles = (groups, SEGMENTS, LANES)
    flipped = (groups, cells, LANES)
    vmem = pl.BlockSpec(memory_space=pltpu.VMEM)
    result = pl.pallas_call(
        functools.partial(kernel, devices, wall_devices, planes),
        out_shape=jax.ShapeDtypeStruct((components, lines, cells), f32),
        in_specs=[pl.BlockSpec(memory_space=pltpu.HBM)] * 3,
        out_specs=vmem,
        scratch_shapes=[
            pltpu.VMEM((components, lines, cells), f32),
            pltpu.VMEM((lines, cells), f32),
            pltpu.VMEM(y_coef.shape, f32),
            pltpu.VMEM((2, 8, cells), f32),
            pltpu.VMEM((2, 8, cells), f32),
            pltpu.VMEM((LANES, cells), f32),
            pltpu.VMEM((every, cells, LANES), f32),
            pltpu.VMEM((components, lines, cells), f32),
            pltpu.VMEM((components,) + flipped, f32),
            pltpu.VMEM((cells, LANES), f32),
            pltpu.VMEM((length, every, SEGMENTS, LANES), f32),
            pltpu.VMEM((length, every, SEGMENTS, LANES), f32),
            pltpu.VMEM((length, every, SEGMENTS, LANES), f32),
            pltpu.VMEM((components, length) + tiles, f32),
            pltpu.VMEM((length, SEGMENTS, LANES), f32),
            pltpu.VMEM((2 * fields, SEGMENTS * 8, LANES), f32),
            pltpu.VMEM((groups, up8(2 * components), LANES), f32),
            pltpu.VMEM((fields,) + flipped, f32),
            pltpu.VMEM((fields, lines, cells), f32),
            pltpu.VMEM((8, -(-rows // LANES) * LANES), f32),
            pltpu.VMEM((rows_a, LANES), f32),
            pltpu.VMEM((rows_b, LANES), f32),
            pltpu.VMEM((8, LANES), f32),
            pltpu.VMEM((peers, rows_a, LANES), f32),
            pltpu.VMEM((peers, rows_b, LANES), f32),
            pltpu.VMEM((peers, 8, LANES), f32),
            pltpu.SemaphoreType.DMA((3,)),
            pltpu.SemaphoreType.DMA((2,)),
            pltpu.SemaphoreType.DMA((2,)),
        ] + [pltpu.SemaphoreType.DMA((peers,))] * 6,
        compiler_params=pltpu.CompilerParams(
            collective_id=0, has_side_effects=True, vmem_limit_bytes=40 * 1024 * 1024
        ),
        name="implicit_lines",
    )(
        pltpu.with_memory_space_constraint(velocity.reshape(components, lines, cells), pltpu.HBM),
        pltpu.with_memory_space_constraint(viscosity.reshape(lines, cells), pltpu.HBM),
        pltpu.with_memory_space_constraint(y_coef, pltpu.HBM),
    )
    return result.reshape(velocity.shape)


def solution(mesh):
    placed = (P(None, None, "wall", "stream"), P(None, "wall", "stream"), P(None, "wall"))
    return jax.shard_map(
        functools.partial(shards, mesh.shape["stream"], mesh.shape["wall"]),
        mesh=mesh,
        in_specs=placed,
        out_specs=P(None, None, "wall", "stream"),
        check_vma=False,
    )
```

```python
import functools

import jax
import jax.numpy as jnp
from jax import lax
from jax.experimental import pallas as pl
from jax.experimental.pallas import tpu as pltpu
from jax.sharding import PartitionSpec as P

SEGMENTS = 8
LANES = 128
MESH = pl.DeviceIdType.MESH


def up8(rows):
    return -(-rows // 8) * 8


def join_matrix(a, b, link):
    a00, a0l, all_ = a
    b00, b0l, bll = b
    gain = link / (1.0 + link * (all_ + b00))
    left = gain * a0l
    right = gain * b0l
    return (a00 - left * a0l, left * b0l, bll - right * b0l), (gain, left, right)


def join_values(a, b, weights):
    _, left, right = weights
    jump = [al - b0 for al, b0 in zip(a[1], b[0])]
    first = [a0 - left * j for a0, j in zip(a[0], jump)]
    last = [bl + right * j for bl, j in zip(b[1], jump)]
    return (first, last), jump


def join_tree(blocks):
    levels = []
    while len(blocks) > 1:
        merged, weights = [], []
        for i in range(0, len(blocks) - 1, 2):
            (ma, fa, la), (mb, fb, lb) = blocks[i], blocks[i + 1]
            m, w = join_matrix(ma, mb, 0.5 * (la + fb))
            merged.append((m, fa, lb))
            weights.append(w)
        if len(blocks) % 2:
            merged.append(blocks[-1])
        levels.append(weights)
        blocks = merged
    return blocks[0], levels


def value_tree(values, levels):
    jumps = []
    for weights in levels:
        merged, jump = [], []
        for i, w in enumerate(weights):
            v, j = join_values(values[2 * i], values[2 * i + 1], w)
            merged.append(v)
            jump.append(j)
        if len(values) % 2:
            merged.append(values[-1])
        jumps.append(jump)
        values = merged
    return values[0], jumps


def down_tree(levels, jumps, inflow, outflow):
    flows = [(inflow, outflow)]
    for depth in reversed(range(len(levels))):
        spread = []
        for i, (gain, left, right) in enumerate(levels[depth]):
            fin, fout = flows[i]
            middle = None
            for term, weight in ((fin, left), (fout, right)):
                if term is not None:
                    part = weight if isinstance(term, float) else term * weight
                    middle = part if middle is None else middle + part
            if jumps is not None:
                part = gain * jumps[depth][i]
                middle = part if middle is None else middle + part
            spread += [(fin, middle), (middle, fout)]
        flows = spread
    return flows


def kernel(devices, wall_devices, planes, vel_hbm, visc_hbm, coef_hbm, out,
           vel, visc, coef, rows_out, rows_in, rim, stiff_t, src, src_t, rim_t, ratio_s, inv_s, head_s,
           y_s, rim_y, seg, flow, sol_t, sol, coef_s, msg_a, msg_b, msg_c, got_a, got_b, got_c, load_sem,
           wall_send, wall_recv, a_send, a_recv, b_send, b_recv, c_send, c_recv):
    components, lines, cells = vel.shape
    rows = lines // planes
    groups = lines // LANES
    length = cells // SEGMENTS
    me = lax.axis_index("stream")
    wall = lax.axis_index("wall")
    has_below = wall > 0
    has_above = wall < wall_devices - 1

    barrier = pltpu.get_barrier_semaphore()
    for d in range(1, devices):
        pl.semaphore_signal(barrier, inc=1, device_id={"stream": lax.rem(me + d, devices)}, device_id_type=MESH)

    @pl.when(has_below)
    def _():
        pl.semaphore_signal(barrier, inc=1, device_id={"wall": wall - 1}, device_id_type=MESH)

    @pl.when(has_above)
    def _():
        pl.semaphore_signal(barrier, inc=1, device_id={"wall": wall + 1}, device_id_type=MESH)

    loads = [
        pltpu.make_async_copy(source, target, load_sem.at[i])
        for i, (source, target) in enumerate(((vel_hbm, vel), (visc_hbm, visc), (coef_hbm, coef)))
    ]
    for load in loads:
        load.start()
    bounds = [(c * planes + p, c, p * rows, (p + 1) * rows - 1) for c in range(components) for p in range(planes)]
    loads[0].wait()
    for at, c, low, high in bounds:
        rows_out[0, at : at + 1, :] = vel[c, high : high + 1, :]
        rows_out[1, at : at + 1, :] = vel[c, low : low + 1, :]
    beside = jnp.where(has_below, 1, 0) + jnp.where(has_above, 1, 0)
    pl.semaphore_wait(barrier, devices - 1 + beside)

    def wall_copy(side, target):
        return pltpu.make_async_remote_copy(
            src_ref=rows_out.at[side], dst_ref=rows_in.at[side],
            send_sem=wall_send.at[side], recv_sem=wall_recv.at[side],
            device_id={"wall": target}, device_id_type=MESH)

    @pl.when(has_above)
    def _():
        wall_copy(0, wall + 1).start()

    @pl.when(has_below)
    def _():
        wall_copy(1, wall - 1).start()

    @pl.when(jnp.logical_not(has_below))
    def _():
        rows_in[0] = jnp.zeros(rows_in.shape[1:], jnp.float32)

    @pl.when(jnp.logical_not(has_above))
    def _():
        rows_in[1] = jnp.zeros(rows_in.shape[1:], jnp.float32)

    loads[1].wait()
    rim[...] = jnp.ones(rim.shape, jnp.float32)
    for at, c, low, high in bounds:
        rim[at : at + 1, :] = visc[low : low + 1, :]
        rim[8 + at : 9 + at, :] = visc[high : high + 1, :]
    for g in range(groups):
        stiff_t[g] = visc[g * LANES : (g + 1) * LANES, :].T
    stiff_t[groups] = rim[...].T

    def ring_copy(d, source, target, send, recv):
        return pltpu.make_async_remote_copy(
            src_ref=source, dst_ref=target.at[d - 1],
            send_sem=send.at[d - 1], recv_sem=recv.at[d - 1],
            device_id={"stream": lax.rem(me + d, devices)}, device_id_type=MESH)

    def at_position(i):
        return pl.ds(i, SEGMENTS, stride=length)

    every = groups + 1

    def put_segments(slot, value, first_group=0):
        for g in range(value.shape[0]):
            seg[slot, pl.ds(first_group + g, SEGMENTS, stride=8), :] = value[g]

    def take_segment(slot, s, span=slice(0, groups)):
        return seg[slot, s * 8 + span.start : s * 8 + span.stop, :]

    one = jnp.ones((every, SEGMENTS, LANES), jnp.float32)
    excess = one
    reach = one
    first_first = jnp.zeros_like(one)
    stiff = stiff_t[:, at_position(0), :]
    first_stiff = stiff
    for i in range(length):
        if i < length - 1:
            following = stiff_t[:, at_position(i + 1), :]
            link = 0.5 * (stiff + following)
            stiff = following
            inv = 1.0 / (excess + link)
            ratio = link * inv
            ratio_s[i] = ratio
        else:
            inv = 1.0 / excess
        head = reach * inv
        inv_s[i] = inv
        head_s[i] = head
        first_first = first_first + head * reach
        if i < length - 1:
            excess = 1.0 + ratio * excess
            reach = reach * ratio
    for slot, value in enumerate((first_first, head, inv, first_stiff, stiff)):
        put_segments(slot, value)
    blocks = []
    for s in range(SEGMENTS):
        v = [take_segment(slot, s, slice(0, every)) for slot in range(5)]
        blocks.append((tuple(v[:3]), v[3], v[4]))
    mine, levels = join_tree(blocks)
    for q, value in enumerate(mine[0] + (mine[1], mine[2])):
        msg_a[q * every : (q + 1) * every, :] = value
    for d in range(1, devices):
        ring_copy(d, msg_a, got_a, a_send, a_recv).start()

    def part(levels, span):
        return [[tuple(w[span] for w in weights) for weights in level] for level in levels]

    main, last = slice(0, groups), slice(groups, every)
    main_levels, rim_levels = part(levels, main), part(levels, last)
    loads[2].wait()
    coef_s[...] = jnp.zeros(coef_s.shape, jnp.float32)
    coef_s[0:2, 0:rows] = coef[...]
    turned = coef_s[...].T
    toward_up = turned[0:rows, 0:1]
    toward_down = turned[0:rows, 1:2]
    keep = 1.0 - toward_up - toward_down
    row_of = lax.broadcasted_iota(jnp.int32, (rows, cells), 0)

    for c in range(components):
        for p in range(planes):
            v = vel[c, p * rows : (p + 1) * rows, :]
            above = jnp.where(row_of == rows - 1, 0.0, pltpu.roll(v, rows - 1, 0))
            below = jnp.where(row_of == 0, 0.0, pltpu.roll(v, 1, 0))
            src[c, p * rows : (p + 1) * rows, :] = v + toward_up * (above - v) - toward_down * (v - below)
        for g in range(groups):
            src_t[c, g] = src[c, g * LANES : (g + 1) * LANES, :].T

    y = [None] * components
    first = [None] * components
    for i in range(length):
        head = head_s[i, main]
        for c in range(components):
            f = src_t[c, :, at_position(i), :]
            y[c] = f if i == 0 else f + ratio_s[i - 1, main] * y[c]
            y_s[c, i] = y[c]
            first[c] = head * y[c] if i == 0 else first[c] + head * y[c]
    inv = inv_s[length - 1, main]
    for c in range(components):
        put_segments(c, first[c])
        put_segments(components + c, inv * y[c])
    values = []
    for s in range(SEGMENTS):
        v = [take_segment(slot, s) for slot in range(2 * components)]
        values.append((v[:components], v[components:]))
    own, jumps = value_tree(values, main_levels)
    for q, value in enumerate(own[0] + own[1]):
        msg_b[q * groups : (q + 1) * groups, :] = value
    for d in range(1, devices):
        ring_copy(d, msg_b, got_b, b_send, b_recv).start()

    @pl.when(has_below)
    def _():
        wall_copy(0, wall).wait_recv()

    @pl.when(has_above)
    def _():
        wall_copy(1, wall).wait_recv()

    rim[0:8, :] = rows_in[0] * turned[0:1, 1:2]
    rim[8:16, :] = rows_in[1] * turned[rows - 1 : rows, 0:1]
    rim_t[...] = rim[...].T
    for i in range(length):
        f = rim_t[at_position(i), :]
        head = head_s[i, groups]
        edge = f if i == 0 else f + ratio_s[i - 1, groups] * edge
        rim_y[i] = edge
        edge_first = head * edge if i == 0 else edge_first + head * edge
    put_segments(0, edge_first[None], groups)
    put_segments(1, (inv_s[length - 1, groups] * edge)[None], groups)
    values = []
    for s in range(SEGMENTS):
        v = [take_segment(slot, s, last) for slot in range(2)]
        values.append((v[:1], v[1:]))
    rim_own, rim_jumps = value_tree(values, rim_levels)
    msg_c[0:1, :] = rim_own[0][0]
    msg_c[1:2, :] = rim_own[1][0]
    for d in range(1, devices):
        ring_copy(d, msg_c, got_c, c_send, c_recv).start()

    fields = components + 2
    zero = jnp.zeros((groups, LANES), jnp.float32)
    unit = jnp.ones((groups, LANES), jnp.float32)
    for f in range(fields):
        if f < components:
            picked = [[j[f] for j in level] for level in jumps]
            flows = down_tree(main_levels, picked, None, None)
        elif f == components:
            flows = down_tree(main_levels, None, 1.0, None)
        else:
            flows = down_tree(main_levels, None, None, 1.0)
        for s, (fin, fout) in enumerate(flows):
            for side, term in enumerate((fin, fout)):
                term = zero if term is None else unit if isinstance(term, float) else term
                seg[2 * f + side, s * 8 : s * 8 + groups, :] = term
    fin, fout = [], []
    for f in range(fields):
        for slot, into in ((2 * f, fin), (2 * f + 1, fout)):
            into.append(jnp.stack([seg[slot, pl.ds(g, SEGMENTS, stride=8), :] for g in range(groups)]))
    picked = [[j[0] for j in level] for level in rim_jumps]
    for s, terms in enumerate(down_tree(rim_levels, picked, None, None)):
        for side, term in enumerate(terms):
            term = jnp.zeros((1, LANES), jnp.float32) if term is None else term
            seg[side, s * 8 + groups : s * 8 + every, :] = term
    rim_fin, rim_fout = (seg[side, pl.ds(groups, SEGMENTS, stride=8), :] for side in range(2))
    for i in reversed(range(length)):
        value = rim_fin * head_s[i, groups] + rim_y[i] * inv_s[i, groups]
        if i < length - 1:
            value = value + ratio_s[i, groups] * edge
        else:
            value = value - rim_fout * inv_s[i, groups]
        edge = value
        rim_t[at_position(i), :] = edge
    rim[...] = rim_t[...].T
    now = [None] * fields
    for i in reversed(range(length)):
        head = head_s[i, main]
        inv = inv_s[i, main]
        if i < length - 1:
            ratio = ratio_s[i, main]
        for f in range(fields):
            value = fin[f] * head
            if f < components:
                value = value + y_s[f, i] * inv
            if i < length - 1:
                value = value + ratio * now[f]
            else:
                value = value - fout[f] * inv
            now[f] = value
            sol_t[f, :, at_position(i), :] = value
    for f in range(fields):
        for g in range(groups):
            sol[f, g * LANES : (g + 1) * LANES, :] = sol_t[f, g].T

    for d in range(1, devices):
        ring_copy(d, msg_a, got_a, a_send, a_recv).wait()
    others = []
    for t in range(1, devices):
        slot = devices - t - 1
        v = [got_a[slot, q * every : (q + 1) * every, :] for q in range(5)]
        others.append((tuple(v[:3]), v[3], v[4]))
    rest, ring_levels = join_tree(others)
    (m00, m0l, mll), m_first, m_last = mine
    (b00, b0l, bll), b_first, b_last = rest
    out_diag = 2.0 / (m_last + b_first) + mll + b00
    in_diag = 2.0 / (b_last + m_first) + bll + m00
    cross = m0l + b0l
    det = 1.0 / (out_diag * in_diag - cross * cross)

    def end_flows(mine_ends, other_ends, span):
        gap_out = mine_ends[1] - other_ends[0]
        gap_in = other_ends[1] - mine_ends[0]
        outflow = (in_diag[span] * gap_out + cross[span] * gap_in) * det[span]
        inflow = (out_diag[span] * gap_in + cross[span] * gap_out) * det[span]
        return inflow, outflow

    for d in range(1, devices):
        ring_copy(d, msg_b, got_b, b_send, b_recv).wait()
    theirs = []
    for t in range(1, devices):
        slot = devices - t - 1
        v = [got_b[slot, q * groups : (q + 1) * groups, :] for q in range(2 * components)]
        theirs.append((v[:components], v[components:]))
    tail, _ = value_tree(theirs, part(ring_levels, main))
    for c in range(components):
        inflow, outflow = end_flows((own[0][c], own[1][c]), (tail[0][c], tail[1][c]), main)
        for g in range(groups):
            flow[g, c : c + 1, :] = inflow[g : g + 1]
            flow[g, components + c : components + c + 1, :] = outflow[g : g + 1]

    for g in range(groups):
        span = slice(g * LANES, (g + 1) * LANES)
        columns = flow[g].T
        from_left = sol[components, span, :]
        from_right = sol[components + 1, span, :]
        for c in range(components):
            out[c, span, :] = (
                sol[c, span, :]
                + columns[:, c : c + 1] * from_left
                + columns[:, components + c : components + c + 1] * from_right
            )

    for d in range(1, devices):
        ring_copy(d, msg_c, got_c, c_send, c_recv).wait()
    theirs = []
    for t in range(1, devices):
        slot = devices - t - 1
        theirs.append(([got_c[slot, 0:1, :]], [got_c[slot, 1:2, :]]))
    tail, _ = value_tree(theirs, part(ring_levels, last))
    inflow, outflow = end_flows((rim_own[0][0], rim_own[1][0]), (tail[0][0], tail[1][0]), last)
    flow[0, 0:1, :] = inflow
    flow[0, 1:2, :] = outflow
    columns = flow[0].T
    for at, c, low, high in bounds:
        for e, r in ((at, low), (8 + at, high)):
            out[c, r : r + 1, :] = (
                out[c, r : r + 1, :]
                + rim[e : e + 1, :]
                + columns[e : e + 1, 0:1] * sol[components, r : r + 1, :]
                + columns[e : e + 1, 1:2] * sol[components + 1, r : r + 1, :]
            )

    @pl.when(has_above)
    def _():
        wall_copy(0, wall + 1).wait_send()

    @pl.when(has_below)
    def _():
        wall_copy(1, wall - 1).wait_send()


def shards(devices, wall_devices, velocity, viscosity, y_coef):
    components, planes, rows, cells = velocity.shape
    lines = planes * rows
    groups = lines // LANES
    length = cells // SEGMENTS
    fields = components + 2
    f32 = jnp.float32
    every = groups + 1
    rows_a, rows_b = up8(5 * every), up8(2 * components * groups)
    peers = devices - 1
    tiles = (groups, SEGMENTS, LANES)
    flipped = (groups, cells, LANES)
    vmem = pl.BlockSpec(memory_space=pltpu.VMEM)
    result = pl.pallas_call(
        functools.partial(kernel, devices, wall_devices, planes),
        out_shape=jax.ShapeDtypeStruct((components, lines, cells), f32),
        in_specs=[pl.BlockSpec(memory_space=pltpu.HBM)] * 3,
        out_specs=vmem,
        scratch_shapes=[
            pltpu.VMEM((components, lines, cells), f32),
            pltpu.VMEM((lines, cells), f32),
            pltpu.VMEM(y_coef.shape, f32),
            pltpu.VMEM((2, 8, cells), f32),
            pltpu.VMEM((2, 8, cells), f32),
            pltpu.VMEM((LANES, cells), f32),
            pltpu.VMEM((every, cells, LANES), f32),
            pltpu.VMEM((components, lines, cells), f32),
            pltpu.VMEM((components,) + flipped, f32),
            pltpu.VMEM((cells, LANES), f32),
            pltpu.VMEM((length, every, SEGMENTS, LANES), f32),
            pltpu.VMEM((length, every, SEGMENTS, LANES), f32),
            pltpu.VMEM((length, every, SEGMENTS, LANES), f32),
            pltpu.VMEM((components, length) + tiles, f32),
            pltpu.VMEM((length, SEGMENTS, LANES), f32),
            pltpu.VMEM((2 * fields, SEGMENTS * 8, LANES), f32),
            pltpu.VMEM((groups, up8(2 * components), LANES), f32),
            pltpu.VMEM((fields,) + flipped, f32),
            pltpu.VMEM((fields, lines, cells), f32),
            pltpu.VMEM((8, -(-rows // LANES) * LANES), f32),
            pltpu.VMEM((rows_a, LANES), f32),
            pltpu.VMEM((rows_b, LANES), f32),
            pltpu.VMEM((2, LANES), f32),
            pltpu.VMEM((peers, rows_a, LANES), f32),
            pltpu.VMEM((peers, rows_b, LANES), f32),
            pltpu.VMEM((peers, 2, LANES), f32),
            pltpu.SemaphoreType.DMA((3,)),
            pltpu.SemaphoreType.DMA((2,)),
            pltpu.SemaphoreType.DMA((2,)),
        ] + [pltpu.SemaphoreType.DMA((peers,))] * 6,
        compiler_params=pltpu.CompilerParams(
            collective_id=0, has_side_effects=True, vmem_limit_bytes=40 * 1024 * 1024
        ),
        name="implicit_lines",
    )(
        pltpu.with_memory_space_constraint(velocity.reshape(components, lines, cells), pltpu.HBM),
        pltpu.with_memory_space_constraint(viscosity.reshape(lines, cells), pltpu.HBM),
        pltpu.with_memory_space_constraint(y_coef, pltpu.HBM),
    )
    return result.reshape(velocity.shape)


def solution(mesh):
    placed = (P(None, None, "wall", "stream"), P(None, "wall", "stream"), P(None, "wall"))
    return jax.shard_map(
        functools.partial(shards, mesh.shape["stream"], mesh.shape["wall"]),
        mesh=mesh,
        in_specs=placed,
        out_specs=P(None, None, "wall", "stream"),
        check_vma=False,
    )
```

```python
import functools

import jax
import jax.numpy as jnp
from jax import lax
from jax.experimental import pallas as pl
from jax.experimental.pallas import tpu as pltpu
from jax.sharding import PartitionSpec as P

SEGMENTS = 8
LANES = 128
MESH = pl.DeviceIdType.MESH


def up8(rows):
    return -(-rows // 8) * 8


def join_matrix(a, b, link):
    a00, a0l, all_ = a
    b00, b0l, bll = b
    gain = link / (1.0 + link * (all_ + b00))
    left = gain * a0l
    right = gain * b0l
    return (a00 - left * a0l, left * b0l, bll - right * b0l), (gain, left, right)


def join_values(a, b, weights):
    _, left, right = weights
    jump = [al - b0 for al, b0 in zip(a[1], b[0])]
    first = [a0 - left * j for a0, j in zip(a[0], jump)]
    last = [bl + right * j for bl, j in zip(b[1], jump)]
    return (first, last), jump


def join_tree(blocks):
    levels = []
    while len(blocks) > 1:
        merged, weights = [], []
        for i in range(0, len(blocks) - 1, 2):
            (ma, fa, la), (mb, fb, lb) = blocks[i], blocks[i + 1]
            m, w = join_matrix(ma, mb, 0.5 * (la + fb))
            merged.append((m, fa, lb))
            weights.append(w)
        if len(blocks) % 2:
            merged.append(blocks[-1])
        levels.append(weights)
        blocks = merged
    return blocks[0], levels


def value_tree(values, levels):
    jumps = []
    for weights in levels:
        merged, jump = [], []
        for i, w in enumerate(weights):
            v, j = join_values(values[2 * i], values[2 * i + 1], w)
            merged.append(v)
            jump.append(j)
        if len(values) % 2:
            merged.append(values[-1])
        jumps.append(jump)
        values = merged
    return values[0], jumps


def down_tree(levels, jumps, inflow, outflow):
    flows = [(inflow, outflow)]
    for depth in reversed(range(len(levels))):
        spread = []
        for i, (gain, left, right) in enumerate(levels[depth]):
            fin, fout = flows[i]
            middle = None
            for term, weight in ((fin, left), (fout, right)):
                if term is not None:
                    part = weight if isinstance(term, float) else term * weight
                    middle = part if middle is None else middle + part
            if jumps is not None:
                part = gain * jumps[depth][i]
                middle = part if middle is None else middle + part
            spread += [(fin, middle), (middle, fout)]
        flows = spread
    return flows


def kernel(devices, wall_devices, planes, vel_hbm, visc_hbm, coef_hbm, out,
           vel, visc, coef, rows_out, rows_in, rim, stiff_t, src, src_t, rim_t, ratio_s, inv_s, head_s,
           y_s, rim_y, seg, flow, sol_t, sol, coef_s, msg_a, msg_b, msg_c, got_a, got_b, got_c, load_sem,
           wall_send, wall_recv, a_send, a_recv, b_send, b_recv, c_send, c_recv):
    components, lines, cells = vel.shape
    rows = lines // planes
    groups = lines // LANES
    length = cells // SEGMENTS
    me = lax.axis_index("stream")
    wall = lax.axis_index("wall")
    has_below = wall > 0
    has_above = wall < wall_devices - 1

    barrier = pltpu.get_barrier_semaphore()
    loads = [
        pltpu.make_async_copy(source, target, load_sem.at[i])
        for i, (source, target) in enumerate(((vel_hbm, vel), (visc_hbm, visc), (coef_hbm, coef)))
    ]
    for load in loads:
        load.start()
    @pl.when(has_below)
    def _():
        pl.semaphore_signal(barrier, inc=1, device_id={"wall": wall - 1}, device_id_type=MESH)

    @pl.when(has_above)
    def _():
        pl.semaphore_signal(barrier, inc=1, device_id={"wall": wall + 1}, device_id_type=MESH)

    for d in range(1, devices):
        pl.semaphore_signal(barrier, inc=1, device_id={"stream": lax.rem(me + d, devices)}, device_id_type=MESH)

    bounds = [(c * planes + p, c, p * rows, (p + 1) * rows - 1) for c in range(components) for p in range(planes)]
    loads[0].wait()
    for at, c, low, high in bounds:
        rows_out[0, at : at + 1, :] = vel[c, high : high + 1, :]
        rows_out[1, at : at + 1, :] = vel[c, low : low + 1, :]
    beside = jnp.where(has_below, 1, 0) + jnp.where(has_above, 1, 0)
    pl.semaphore_wait(barrier, devices - 1 + beside)

    def wall_copy(side, target):
        return pltpu.make_async_remote_copy(
            src_ref=rows_out.at[side], dst_ref=rows_in.at[side],
            send_sem=wall_send.at[side], recv_sem=wall_recv.at[side],
            device_id={"wall": target}, device_id_type=MESH)

    @pl.when(has_above)
    def _():
        wall_copy(0, wall + 1).start()

    @pl.when(has_below)
    def _():
        wall_copy(1, wall - 1).start()

    @pl.when(jnp.logical_not(has_below))
    def _():
        rows_in[0] = jnp.zeros(rows_in.shape[1:], jnp.float32)

    @pl.when(jnp.logical_not(has_above))
    def _():
        rows_in[1] = jnp.zeros(rows_in.shape[1:], jnp.float32)

    loads[1].wait()
    rim[...] = jnp.ones(rim.shape, jnp.float32)
    for at, c, low, high in bounds:
        rim[at : at + 1, :] = visc[low : low + 1, :]
        rim[8 + at : 9 + at, :] = visc[high : high + 1, :]
    for g in range(groups):
        stiff_t[g] = visc[g * LANES : (g + 1) * LANES, :].T
    stiff_t[groups] = rim[...].T

    def ring_copy(d, source, target, send, recv):
        return pltpu.make_async_remote_copy(
            src_ref=source, dst_ref=target.at[d - 1],
            send_sem=send.at[d - 1], recv_sem=recv.at[d - 1],
            device_id={"stream": lax.rem(me + d, devices)}, device_id_type=MESH)

    def at_position(i):
        return pl.ds(i, SEGMENTS, stride=length)

    every = groups + 1

    def put_segments(slot, value, first_group=0):
        for g in range(value.shape[0]):
            seg[slot, pl.ds(first_group + g, SEGMENTS, stride=8), :] = value[g]

    def take_segment(slot, s, span=slice(0, groups)):
        return seg[slot, s * 8 + span.start : s * 8 + span.stop, :]

    one = jnp.ones((every, SEGMENTS, LANES), jnp.float32)
    excess = one
    reach = one
    first_first = jnp.zeros_like(one)
    stiff = stiff_t[:, at_position(0), :]
    first_stiff = stiff
    for i in range(length):
        if i < length - 1:
            following = stiff_t[:, at_position(i + 1), :]
            link = 0.5 * (stiff + following)
            stiff = following
            inv = 1.0 / (excess + link)
            ratio = link * inv
            ratio_s[i] = ratio
        else:
            inv = 1.0 / excess
        head = reach * inv
        inv_s[i] = inv
        head_s[i] = head
        first_first = first_first + head * reach
        if i < length - 1:
            excess = 1.0 + ratio * excess
            reach = reach * ratio
    for slot, value in enumerate((first_first, head, inv, first_stiff, stiff)):
        put_segments(slot, value)
    blocks = []
    for s in range(SEGMENTS):
        v = [take_segment(slot, s, slice(0, every)) for slot in range(5)]
        blocks.append((tuple(v[:3]), v[3], v[4]))
    mine, levels = join_tree(blocks)
    for q, value in enumerate(mine[0] + (mine[1], mine[2])):
        msg_a[q * every : (q + 1) * every, :] = value
    for d in range(1, devices):
        ring_copy(d, msg_a, got_a, a_send, a_recv).start()

    def part(levels, span):
        return [[tuple(w[span] for w in weights) for weights in level] for level in levels]

    main, last = slice(0, groups), slice(groups, every)
    main_levels, rim_levels = part(levels, main), part(levels, last)
    loads[2].wait()
    coef_s[...] = jnp.zeros(coef_s.shape, jnp.float32)
    coef_s[0:2, 0:rows] = coef[...]
    turned = coef_s[...].T
    toward_up = turned[0:rows, 0:1]
    toward_down = turned[0:rows, 1:2]
    keep = 1.0 - toward_up - toward_down
    row_of = lax.broadcasted_iota(jnp.int32, (rows, cells), 0)

    for c in range(components):
        for p in range(planes):
            v = vel[c, p * rows : (p + 1) * rows, :]
            above = jnp.where(row_of == rows - 1, 0.0, pltpu.roll(v, rows - 1, 0))
            below = jnp.where(row_of == 0, 0.0, pltpu.roll(v, 1, 0))
            src[c, p * rows : (p + 1) * rows, :] = v + toward_up * (above - v) - toward_down * (v - below)
        for g in range(groups):
            src_t[c, g] = src[c, g * LANES : (g + 1) * LANES, :].T

    y = [None] * components
    first = [None] * components
    for i in range(length):
        head = head_s[i, main]
        for c in range(components):
            f = src_t[c, :, at_position(i), :]
            y[c] = f if i == 0 else f + ratio_s[i - 1, main] * y[c]
            y_s[c, i] = y[c]
            first[c] = head * y[c] if i == 0 else first[c] + head * y[c]
    inv = inv_s[length - 1, main]
    for c in range(components):
        put_segments(c, first[c])
        put_segments(components + c, inv * y[c])
    values = []
    for s in range(SEGMENTS):
        v = [take_segment(slot, s) for slot in range(2 * components)]
        values.append((v[:components], v[components:]))
    own, jumps = value_tree(values, main_levels)
    for q, value in enumerate(own[0] + own[1]):
        msg_b[q * groups : (q + 1) * groups, :] = value
    for d in range(1, devices):
        ring_copy(d, msg_b, got_b, b_send, b_recv).start()

    @pl.when(has_below)
    def _():
        wall_copy(0, wall).wait_recv()

    @pl.when(has_above)
    def _():
        wall_copy(1, wall).wait_recv()

    rim[0:8, :] = rows_in[0] * turned[0:1, 1:2]
    rim[8:16, :] = rows_in[1] * turned[rows - 1 : rows, 0:1]
    rim_t[...] = rim[...].T
    for i in range(length):
        f = rim_t[at_position(i), :]
        head = head_s[i, groups]
        edge = f if i == 0 else f + ratio_s[i - 1, groups] * edge
        rim_y[i] = edge
        edge_first = head * edge if i == 0 else edge_first + head * edge
    put_segments(0, edge_first[None], groups)
    put_segments(1, (inv_s[length - 1, groups] * edge)[None], groups)
    values = []
    for s in range(SEGMENTS):
        v = [take_segment(slot, s, last) for slot in range(2)]
        values.append((v[:1], v[1:]))
    rim_own, rim_jumps = value_tree(values, rim_levels)
    msg_c[0:1, :] = rim_own[0][0]
    msg_c[1:2, :] = rim_own[1][0]
    for d in range(1, devices):
        ring_copy(d, msg_c, got_c, c_send, c_recv).start()

    fields = components + 2
    zero = jnp.zeros((groups, LANES), jnp.float32)
    unit = jnp.ones((groups, LANES), jnp.float32)
    for f in range(fields):
        if f < components:
            picked = [[j[f] for j in level] for level in jumps]
            flows = down_tree(main_levels, picked, None, None)
        elif f == components:
            flows = down_tree(main_levels, None, 1.0, None)
        else:
            flows = down_tree(main_levels, None, None, 1.0)
        for s, (fin, fout) in enumerate(flows):
            for side, term in enumerate((fin, fout)):
                term = zero if term is None else unit if isinstance(term, float) else term
                seg[2 * f + side, s * 8 : s * 8 + groups, :] = term
    fin, fout = [], []
    for f in range(fields):
        for slot, into in ((2 * f, fin), (2 * f + 1, fout)):
            into.append(jnp.stack([seg[slot, pl.ds(g, SEGMENTS, stride=8), :] for g in range(groups)]))
    picked = [[j[0] for j in level] for level in rim_jumps]
    for s, terms in enumerate(down_tree(rim_levels, picked, None, None)):
        for side, term in enumerate(terms):
            term = jnp.zeros((1, LANES), jnp.float32) if term is None else term
            seg[side, s * 8 + groups : s * 8 + every, :] = term
    rim_fin, rim_fout = (seg[side, pl.ds(groups, SEGMENTS, stride=8), :] for side in range(2))
    for i in reversed(range(length)):
        value = rim_fin * head_s[i, groups] + rim_y[i] * inv_s[i, groups]
        if i < length - 1:
            value = value + ratio_s[i, groups] * edge
        else:
            value = value - rim_fout * inv_s[i, groups]
        edge = value
        rim_t[at_position(i), :] = edge
    rim[...] = rim_t[...].T
    now = [None] * fields
    for i in reversed(range(length)):
        head = head_s[i, main]
        inv = inv_s[i, main]
        if i < length - 1:
            ratio = ratio_s[i, main]
        for f in range(fields):
            value = fin[f] * head
            if f < components:
                value = value + y_s[f, i] * inv
            if i < length - 1:
                value = value + ratio * now[f]
            else:
                value = value - fout[f] * inv
            now[f] = value
            sol_t[f, :, at_position(i), :] = value
    for f in range(fields):
        for g in range(groups):
            sol[f, g * LANES : (g + 1) * LANES, :] = sol_t[f, g].T

    for d in range(1, devices):
        ring_copy(d, msg_a, got_a, a_send, a_recv).wait()
    others = []
    for t in range(1, devices):
        slot = devices - t - 1
        v = [got_a[slot, q * every : (q + 1) * every, :] for q in range(5)]
        others.append((tuple(v[:3]), v[3], v[4]))
    rest, ring_levels = join_tree(others)
    (m00, m0l, mll), m_first, m_last = mine
    (b00, b0l, bll), b_first, b_last = rest
    out_diag = 2.0 / (m_last + b_first) + mll + b00
    in_diag = 2.0 / (b_last + m_first) + bll + m00
    cross = m0l + b0l
    det = 1.0 / (out_diag * in_diag - cross * cross)

    def end_flows(mine_ends, other_ends, span):
        gap_out = mine_ends[1] - other_ends[0]
        gap_in = other_ends[1] - mine_ends[0]
        outflow = (in_diag[span] * gap_out + cross[span] * gap_in) * det[span]
        inflow = (out_diag[span] * gap_in + cross[span] * gap_out) * det[span]
        return inflow, outflow

    for d in range(1, devices):
        ring_copy(d, msg_b, got_b, b_send, b_recv).wait()
    theirs = []
    for t in range(1, devices):
        slot = devices - t - 1
        v = [got_b[slot, q * groups : (q + 1) * groups, :] for q in range(2 * components)]
        theirs.append((v[:components], v[components:]))
    tail, _ = value_tree(theirs, part(ring_levels, main))
    for c in range(components):
        inflow, outflow = end_flows((own[0][c], own[1][c]), (tail[0][c], tail[1][c]), main)
        for g in range(groups):
            flow[g, c : c + 1, :] = inflow[g : g + 1]
            flow[g, components + c : components + c + 1, :] = outflow[g : g + 1]

    for g in range(groups):
        span = slice(g * LANES, (g + 1) * LANES)
        columns = flow[g].T
        from_left = sol[components, span, :]
        from_right = sol[components + 1, span, :]
        for c in range(components):
            out[c, span, :] = (
                sol[c, span, :]
                + columns[:, c : c + 1] * from_left
                + columns[:, components + c : components + c + 1] * from_right
            )

    for d in range(1, devices):
        ring_copy(d, msg_c, got_c, c_send, c_recv).wait()
    theirs = []
    for t in range(1, devices):
        slot = devices - t - 1
        theirs.append(([got_c[slot, 0:1, :]], [got_c[slot, 1:2, :]]))
    tail, _ = value_tree(theirs, part(ring_levels, last))
    inflow, outflow = end_flows((rim_own[0][0], rim_own[1][0]), (tail[0][0], tail[1][0]), last)
    flow[0, 0:1, :] = inflow
    flow[0, 1:2, :] = outflow
    columns = flow[0].T
    for at, c, low, high in bounds:
        for e, r in ((at, low), (8 + at, high)):
            out[c, r : r + 1, :] = (
                out[c, r : r + 1, :]
                + rim[e : e + 1, :]
                + columns[e : e + 1, 0:1] * sol[components, r : r + 1, :]
                + columns[e : e + 1, 1:2] * sol[components + 1, r : r + 1, :]
            )

    @pl.when(has_above)
    def _():
        wall_copy(0, wall + 1).wait_send()

    @pl.when(has_below)
    def _():
        wall_copy(1, wall - 1).wait_send()


def shards(devices, wall_devices, velocity, viscosity, y_coef):
    components, planes, rows, cells = velocity.shape
    lines = planes * rows
    groups = lines // LANES
    length = cells // SEGMENTS
    fields = components + 2
    f32 = jnp.float32
    every = groups + 1
    rows_a, rows_b = up8(5 * every), up8(2 * components * groups)
    peers = devices - 1
    tiles = (groups, SEGMENTS, LANES)
    flipped = (groups, cells, LANES)
    vmem = pl.BlockSpec(memory_space=pltpu.VMEM)
    result = pl.pallas_call(
        functools.partial(kernel, devices, wall_devices, planes),
        out_shape=jax.ShapeDtypeStruct((components, lines, cells), f32),
        in_specs=[pl.BlockSpec(memory_space=pltpu.HBM)] * 3,
        out_specs=vmem,
        scratch_shapes=[
            pltpu.VMEM((components, lines, cells), f32),
            pltpu.VMEM((lines, cells), f32),
            pltpu.VMEM(y_coef.shape, f32),
            pltpu.VMEM((2, 8, cells), f32),
            pltpu.VMEM((2, 8, cells), f32),
            pltpu.VMEM((LANES, cells), f32),
            pltpu.VMEM((every, cells, LANES), f32),
            pltpu.VMEM((components, lines, cells), f32),
            pltpu.VMEM((components,) + flipped, f32),
            pltpu.VMEM((cells, LANES), f32),
            pltpu.VMEM((length, every, SEGMENTS, LANES), f32),
            pltpu.VMEM((length, every, SEGMENTS, LANES), f32),
            pltpu.VMEM((length, every, SEGMENTS, LANES), f32),
            pltpu.VMEM((components, length) + tiles, f32),
            pltpu.VMEM((length, SEGMENTS, LANES), f32),
            pltpu.VMEM((2 * fields, SEGMENTS * 8, LANES), f32),
            pltpu.VMEM((groups, up8(2 * components), LANES), f32),
            pltpu.VMEM((fields,) + flipped, f32),
            pltpu.VMEM((fields, lines, cells), f32),
            pltpu.VMEM((8, -(-rows // LANES) * LANES), f32),
            pltpu.VMEM((rows_a, LANES), f32),
            pltpu.VMEM((rows_b, LANES), f32),
            pltpu.VMEM((2, LANES), f32),
            pltpu.VMEM((peers, rows_a, LANES), f32),
            pltpu.VMEM((peers, rows_b, LANES), f32),
            pltpu.VMEM((peers, 2, LANES), f32),
            pltpu.SemaphoreType.DMA((3,)),
            pltpu.SemaphoreType.DMA((2,)),
            pltpu.SemaphoreType.DMA((2,)),
        ] + [pltpu.SemaphoreType.DMA((peers,))] * 6,
        compiler_params=pltpu.CompilerParams(
            collective_id=0, has_side_effects=True, vmem_limit_bytes=40 * 1024 * 1024
        ),
        name="implicit_lines",
    )(
        pltpu.with_memory_space_constraint(velocity.reshape(components, lines, cells), pltpu.HBM),
        pltpu.with_memory_space_constraint(viscosity.reshape(lines, cells), pltpu.HBM),
        pltpu.with_memory_space_constraint(y_coef, pltpu.HBM),
    )
    return result.reshape(velocity.shape)


def solution(mesh):
    placed = (P(None, None, "wall", "stream"), P(None, "wall", "stream"), P(None, "wall"))
    return jax.shard_map(
        functools.partial(shards, mesh.shape["stream"], mesh.shape["wall"]),
        mesh=mesh,
        in_specs=placed,
        out_specs=P(None, None, "wall", "stream"),
        check_vma=False,
    )
```
